256 devices in a mesh: noise: 8 (over x, y_hi), row: 4 (over y_lo, core), col: 8 (over z).
Axes of the slice: x: 4, y: 4 (y_hi: 2, y_lo: 2; y = y_hi * 2 + y_lo), z: 8, core: 2. Of those that a mesh axis runs over, the one named last changes fastest.
Arguments:
- image: bfloat16 [1024, 256, 128], P(('noise', 'row'), 'col'), parts along dimension 0, may hold values from -6 to 6
- noise_level: int32 [8], P('noise'), parts along dimension 0, may hold values from 0 to 7
- cond_table: float32 [8, 256], replicated, may hold values from -6 to 6
- ada_fine: float32 [256, 128], replicated, may hold values from -0.375 to 0.375
- fine_qkv: bfloat16 [128, 384], replicated, may hold values from -0.5 to 0.5
- fine_scale: float32 [2], replicated, may hold values from 4 to 16
- fine_out_w: bfloat16 [128, 128], replicated, may hold values from -0.5 to 0.5
- fine_post: float32 [128], replicated, may hold values from 0.1 to 1.9
- merge_w: bfloat16 [512, 256], replicated, may hold values from -0.25 to 0.25
- coarse_in_w: bfloat16 [256, 1024], replicated, may hold values from -0.375 to 0.375
- ada_coarse: float32 [256, 1024], replicated, may hold values from -0.375 to 0.375
- coarse_qkv: bfloat16 [3, 1024, 1024], P(None, None, 'col'), may hold values from -0.1875 to 0.1875
- coarse_scale: float32 [16], P('col'), may hold values from 4 to 16
- coarse_out_w: bfloat16 [1024, 1024], P('col'), may hold values from -0.1875 to 0.1875
- coarse_post: float32 [1024], replicated, may hold values from 0.1 to 1.9
Outputs:
- fine_out: bfloat16 [1024, 256, 128], P(('noise', 'row'), 'col'), parts along dimension 0
- coarse_out: bfloat16 [64, 16, 1024], P(('noise', 'row'), 'col'), parts along dimension 0
The draws below stay inside these ranges and needn't reach their ends.
There are 8 independent parts, one for each index of `noise`. The reference program is written for one: setup_inputs(seed, part) draws one part's arguments, and reference() takes and returns one part's arrays. A program takes and returns all parts, laid end to end along the dimension named above; an argument that names none is the same for every part. Nothing has to cross between parts.
All inputs are finite; a program needn't handle non-finite values.
Results may differ from the reference program's by a relative error of at most 0.035.
Values may be sent and summed in bfloat16 or wider, within the bound.
No kernel may reach another device: no remote copies, remote signals or barrier semaphores. Data moves between devices by JAX's collectives and lax.ppermute only.
A program may use at most 128 MiB of HBM per device.

```python
import math
import jax
import jax.numpy as jnp
from jax import lax

D = 128
HEAD = 64
HF = 2
DM = 256
DC = 1024
HC = 16
COND = 256
NLEV = 8
TILE = 32
POOL = 8
NR = 128
NC = 256
PR = 8
PC = 16


def block_scale(stream_key, dims, split, low, high):
    gain, own = 1.0, jax.random.fold_in(stream_key, 6)
    for axis_at, parts in split:
        steps = jnp.exp(jax.random.uniform(jax.random.fold_in(own, axis_at), (parts,), jnp.float32, low / len(split), high / len(split)))
        gain = gain * jnp.repeat(steps, dims[axis_at] // parts).reshape([-1 if axis == axis_at else 1 for axis in range(len(dims))])
    return gain


def centred(own_key, extent, spread, most, shards=(), held_as=jnp.bfloat16):
    values = spread * jax.random.normal(own_key, extent, jnp.float32)
    if shards:
        values = values * block_scale(own_key, extent, shards, -0.22, 0.18)
    return jnp.clip(values, -most, most).astype(held_as)


def setup_inputs(seed: int = 0, part: int = 0) -> dict:
    splits = jax.random.split(jax.random.key(seed), 16)
    part_keys = jax.random.split(jax.random.fold_in(splits[15], part), 16)
    image = centred(part_keys[0], (NR, NC, D), 1.0, 6.0, ((0, 4), (1, 8)))
    noise_level = jax.random.randint(part_keys[1], (1,), 0, NLEV).astype(jnp.int32)
    cond_table = centred(splits[2], (NLEV, COND), 1.0, 6.0, (), jnp.float32)
    ada_fine = centred(splits[3], (COND, D), COND ** -0.5, 0.375, (), jnp.float32)
    fine_qkv = centred(splits[4], (D, 3 * D), D ** -0.5, 0.5)
    fine_scale = jnp.clip(jnp.exp(jax.random.uniform(splits[5], (HF,), jnp.float32, math.log(4.0), math.log(16.0))), 4.0, 16.0)
    fine_out_w = centred(splits[6], (D, D), D ** -0.5, 0.5)
    fine_post = jnp.clip(1.0 + 0.18 * jax.random.normal(splits[7], (D,), jnp.float32), 0.1, 1.9)
    merge_w = centred(splits[8], (4 * D, DM), (4 * D) ** -0.5, 0.25)
    coarse_in_w = centred(splits[9], (DM, DC), DM ** -0.5, 0.375)
    ada_coarse = centred(splits[10], (COND, DC), COND ** -0.5, 0.375, (), jnp.float32)
    coarse_qkv = centred(splits[11], (3, DC, DC), DC ** -0.5, 0.1875, ((2, 8),))
    coarse_scale = jnp.clip(jnp.exp(math.log(16.0) - 1.3862944 * jax.random.uniform(splits[12], (HC,), jnp.float32) ** block_scale(splits[12], (HC,), ((0, 8),), -0.2, 0.2)), 4.0, 16.0)
    coarse_out_w = centred(splits[13], (DC, DC), DC ** -0.5, 0.1875, ((0, 8),))
    coarse_post = jnp.clip(1.0 + 0.18 * jax.random.normal(splits[14], (DC,), jnp.float32), 0.1, 1.9)
    return {"image": image, "noise_level": noise_level, "cond_table": cond_table, "ada_fine": ada_fine, "fine_qkv": fine_qkv, "fine_scale": fine_scale, "fine_out_w": fine_out_w, "fine_post": fine_post, "merge_w": merge_w, "coarse_in_w": coarse_in_w, "ada_coarse": ada_coarse, "coarse_qkv": coarse_qkv, "coarse_scale": coarse_scale, "coarse_out_w": coarse_out_w, "coarse_post": coarse_post}


def rms(value):
    return value * lax.rsqrt(lax.optimization_barrier(jnp.mean(value * value, axis=-1, keepdims=True)) + 1e-06)

def cosine(value, heads):
    shaped = value.reshape(value.shape[:-1] + (heads, HEAD))
    return rms(shaped).reshape(value.shape)

def attend(queries, keys, values, valid, scale, heads):
    results = []
    for head in range(heads):
        low = head * HEAD
        scores = jnp.dot(queries[:, low:low + HEAD], keys[:, low:low + HEAD].T, preferred_element_type=jnp.float32)
        scores = scores * (scale[head] / HEAD)
        if valid is not None:
            scores = jnp.where(valid[None, :], scores, -jnp.inf)
        top = lax.optimization_barrier(jnp.max(scores, axis=-1, keepdims=True))
        expo = jnp.exp(scores - top)
        if valid is not None:
            expo = jnp.where(valid[None, :], expo, 0.0)
        weights = (expo / lax.optimization_barrier(jnp.sum(expo, axis=-1, keepdims=True))).astype(jnp.bfloat16)
        results.append(jnp.dot(weights, values[:, low:low + HEAD], preferred_element_type=jnp.float32))
    return jnp.concatenate(results, axis=-1).astype(jnp.bfloat16)

def reference(image, noise_level, cond_table, ada_fine, fine_qkv, fine_scale, fine_out_w, fine_post, merge_w, coarse_in_w, ada_coarse, coarse_qkv, coarse_scale, coarse_out_w, coarse_post):
    highest = lax.Precision.HIGHEST
    levels = jnp.arange(NLEV, dtype=jnp.int32)
    hot = (levels == noise_level[0]).astype(jnp.float32)
    cond = jnp.dot(hot, cond_table, precision=highest)
    fine_gain = 1.0 + jnp.dot(cond, ada_fine, precision=highest)
    coarse_gain = 1.0 + jnp.dot(cond, ada_coarse, precision=highest)
    xfull = image.astype(jnp.float32)
    xn = (rms(xfull) * fine_gain).astype(jnp.bfloat16)
    qkv = jnp.dot(xn.reshape(-1, D), fine_qkv, preferred_element_type=jnp.float32).reshape(NR, NC, 3 * D)
    queries = cosine(qkv[..., :D], HF).astype(jnp.bfloat16)
    keys = cosine(qkv[..., D:2 * D], HF).astype(jnp.bfloat16)
    values = qkv[..., 2 * D:].astype(jnp.bfloat16)
    keys_pad = jnp.pad(keys, ((TILE, TILE), (TILE, TILE), (0, 0)))
    values_pad = jnp.pad(values, ((TILE, TILE), (TILE, TILE), (0, 0)))
    row_ids = jnp.arange(NR + 2 * TILE, dtype=jnp.int32) - TILE
    col_ids = jnp.arange(NC + 2 * TILE, dtype=jnp.int32) - TILE
    inside = ((row_ids >= 0) & (row_ids < NR))[:, None] & ((col_ids >= 0) & (col_ids < NC))[None, :]
    tile_cols = NC // TILE
    tile_rows = NR // TILE

    def one_tile(index):
        trow = (index // tile_cols).astype(jnp.int32)
        tcol = (index % tile_cols).astype(jnp.int32)
        zero = jnp.zeros((), jnp.int32)
        q_tile = lax.dynamic_slice(queries, (trow * TILE, tcol * TILE, zero), (TILE, TILE, D)).reshape(TILE * TILE, D)
        k_win = lax.dynamic_slice(keys_pad, (trow * TILE, tcol * TILE, zero), (3 * TILE, 3 * TILE, D)).reshape(-1, D)
        v_win = lax.dynamic_slice(values_pad, (trow * TILE, tcol * TILE, zero), (3 * TILE, 3 * TILE, D)).reshape(-1, D)
        valid = lax.dynamic_slice(inside, (trow * TILE, tcol * TILE), (3 * TILE, 3 * TILE)).reshape(-1)
        return attend(q_tile, k_win, v_win, valid, fine_scale, HF)
    tiles = lax.map(one_tile, jnp.arange(tile_rows * tile_cols, dtype=jnp.int32))
    attended = tiles.reshape(tile_rows, tile_cols, TILE, TILE, D).transpose(0, 2, 1, 3, 4).reshape(NR, NC, D)
    branch = jnp.dot(attended.reshape(-1, D), fine_out_w, preferred_element_type=jnp.float32).reshape(NR, NC, D)
    fine_out = (xfull + rms(branch) * fine_post).astype(jnp.bfloat16)
    blocks = fine_out.reshape(NR // 2, 2, NC // 2, 2, D).transpose(0, 2, 1, 3, 4).reshape(-1, 4 * D)
    merged = jnp.dot(blocks, merge_w, preferred_element_type=jnp.float32).astype(jnp.bfloat16)
    merged = merged.reshape(PR, POOL, PC, POOL, DM).astype(jnp.float32)
    pooled = lax.optimization_barrier(jnp.mean(merged, axis=(1, 3))).astype(jnp.bfloat16).reshape(-1, DM)
    coarse_in = jnp.dot(pooled, coarse_in_w, preferred_element_type=jnp.float32)
    cn = (rms(coarse_in) * coarse_gain).astype(jnp.bfloat16)
    qc = cosine(jnp.dot(cn, coarse_qkv[0], preferred_element_type=jnp.float32), HC).astype(jnp.bfloat16)
    kc = cosine(jnp.dot(cn, coarse_qkv[1], preferred_element_type=jnp.float32), HC).astype(jnp.bfloat16)
    vc = jnp.dot(cn, coarse_qkv[2], preferred_element_type=jnp.float32).astype(jnp.bfloat16)
    coarse_attended = attend(qc, kc, vc, None, coarse_scale, HC)
    coarse_branch = jnp.dot(coarse_attended, coarse_out_w, preferred_element_type=jnp.float32)
    coarse_out = (coarse_in + rms(coarse_branch) * coarse_post).astype(jnp.bfloat16).reshape(PR, PC, DC)
    return (fine_out, coarse_out)
```

```python
import functools

import jax
import jax.numpy as jnp
from jax import lax
from jax.experimental import pallas as pl
from jax.experimental.pallas import tpu as pltpu
from jax.sharding import PartitionSpec as P

HEAD = 64
POOL = 8
EPS = 1e-06
LOG2E = 1.4426950408889634
QCHUNK = 256
VMEM_LIMIT = 40 * 1024 * 1024
NT = (((1,), (1,)), ((), ()))
NN = (((1,), (0,)), ((), ()))
F32 = jnp.float32
BF16 = jnp.bfloat16


def mm(a, b, dims=NN):
    return lax.dot_general(a, b, dims, preferred_element_type=F32)


def rms_rows(value):
    return value * lax.rsqrt(jnp.mean(value * value, axis=-1, keepdims=True) + EPS)


def head_means(value):
    width = value.shape[1]
    i = lax.broadcasted_iota(jnp.int32, (width, width), 0) // HEAD
    j = lax.broadcasted_iota(jnp.int32, (width, width), 1) // HEAD
    ones = jnp.where(i == j, 1.0 / HEAD, 0.0).astype(BF16)
    return mm((value * value).astype(BF16), ones)


def low_lanes(shape):
    return lax.broadcasted_iota(jnp.int32, shape, 1) < HEAD


def level_row(level_ref, table_ref):
    table = table_ref[...]
    ids = lax.broadcasted_iota(jnp.int32, table.shape, 0)
    return jnp.sum(jnp.where(ids == level_ref[0], table, 0.0), axis=0, keepdims=True)


def gain_row(cond, ada_ref):
    return 1.0 + lax.dot_general(
        cond, ada_ref[...], NN, precision=lax.Precision.HIGHEST, preferred_element_type=F32
    )


def tile_kv(x, gain, wkv, valid):
    width = x.shape[1]
    xn = (rms_rows(x.astype(F32)) * gain).astype(BF16)
    proj = mm(xn, wkv)
    k = proj[:, :width]
    k = (k * lax.rsqrt(head_means(k) + EPS)).astype(BF16)
    v = proj[:, width:]
    low = low_lanes(v.shape)
    v0 = jnp.where(low, v, valid).astype(BF16)
    v1 = jnp.where(low, valid, v).astype(BF16)
    return xn, k, v0, v1


def attend_tile(q_refs, k, vs, acc_refs, first):
    for start in range(0, q_refs[0].shape[0], QCHUNK):
        rows = pl.ds(start, QCHUNK)
        for q_ref, v, acc_ref in zip(q_refs, vs, acc_refs):
            p = jnp.exp2(mm(q_ref[rows, :], k, NT)).astype(BF16)
            part = mm(p, v)
            if first:
                acc_ref[rows, :] = part
            else:
                acc_ref[rows, :] += part


def own_kernel(level, scale, x, table, ada, wqkv, q0, q1, acc0, acc1, gain_out):
    width = x.shape[1]
    gain = gain_row(level_row(level, table), ada)
    gain_out[...] = gain
    xn, k, v0, v1 = tile_kv(x[...], gain, wqkv[:, width:], 1.0)
    q = mm(xn, wqkv[:, :width])
    low = low_lanes(q.shape)
    factor = jnp.where(low, scale[0], scale[1]) * (LOG2E / HEAD)
    q = q * lax.rsqrt(head_means(q) + EPS) * factor
    q0[...] = jnp.where(low, q, 0.0).astype(BF16)
    q1[...] = jnp.where(low, 0.0, q).astype(BF16)
    attend_tile((q0, q1), k, (v0, v1), (acc0, acc1), True)


def edge_flags():
    row, col = lax.axis_index("row"), lax.axis_index("col")
    row_ok = (row > 0) & (row < lax.axis_size("row") - 1)
    col_ok = (col > 0) & (col < lax.axis_size("col") - 1)
    return jnp.where(row_ok, 1.0, 0.0), jnp.where(col_ok, 1.0, 0.0)


def more_tiles(which, tiles, gain, wqkv, q_refs, acc_refs):
    width = wqkv.shape[0]
    row_ok, col_ok = edge_flags()
    flags = {"col": (1.0, col_ok), "near": (1.0, 1.0, col_ok), "far": (row_ok, row_ok, row_ok * col_ok)}
    for at, valid in enumerate(flags[which]):
        _, k, v0, v1 = tile_kv(tiles[at][...], gain[...], wqkv[:, width:], valid)
        attend_tile(q_refs, k, (v0, v1), acc_refs, False)


def col_kernel(a, b, gain, wqkv, q0, q1, acc0_in, acc1_in, acc0, acc1):
    acc0[...] = acc0_in[...]
    acc1[...] = acc1_in[...]
    more_tiles("col", (a, b), gain, wqkv, (q0, q1), (acc0, acc1))


def near_kernel(tiles, gain, wqkv, q0, q1, acc0_in, acc1_in, acc0, acc1):
    acc0[...] = acc0_in[...]
    acc1[...] = acc1_in[...]
    more_tiles("near", [tiles.at[i] for i in range(3)], gain, wqkv, (q0, q1), (acc0, acc1))


def far_kernel(
    tiles, gain, wqkv, q0, q1, acc0_in, acc1_in, x, wout, post, wmerge, out, pooled, acc0, acc1
):
    acc0[...] = acc0_in[...]
    acc1[...] = acc1_in[...]
    more_tiles("far", [tiles.at[i] for i in range(3)], gain, wqkv, (q0, q1), (acc0, acc1))
    tokens, width = x.shape
    low = low_lanes((tokens, width))
    a0, a1 = acc0[...], acc1[...]
    sums = pltpu.roll(jnp.where(low, a1, a0), HEAD, 1)
    attended = (jnp.where(low, a0, a1) / sums).astype(BF16)
    branch = mm(attended, wout[...])
    result = (x[...].astype(F32) + rms_rows(branch) * post[...]).astype(BF16)
    out[...] = result
    side = 32
    group = lax.broadcasted_iota(jnp.int32, (16, tokens), 0)
    token = lax.broadcasted_iota(jnp.int32, (16, tokens), 1)
    i, j = token // side, token % side
    place = ((i % 2) * 2 + j % 2) * 4 + (i // (2 * POOL)) * 2 + j // (2 * POOL)
    pick = jnp.where(group == place, 1.0 / (POOL * POOL), 0.0).astype(BF16)
    means = mm(pick, result)
    high = means.astype(BF16)
    rest = (means - high.astype(F32)).astype(BF16)
    total = jnp.zeros((4, wmerge.shape[1]), F32)
    for part in range(4):
        w = wmerge[pl.ds(part * width, width), :]
        at = slice(4 * part, 4 * part + 4)
        total += mm(high[at], w) + mm(rest[at], w)
    pooled[...] = jnp.broadcast_to(total.astype(BF16)[None], pooled.shape)


def coarse_kernel(
    level, scale, tokens, table, ada, win, wqkv, wout, own, part_out, coarse_in_out, cn_ref, in_ref
):
    row, col = lax.axis_index("row"), lax.axis_index("col")
    count = tokens.shape[0]
    rows_each = count // lax.axis_size("row")
    own_each = rows_each // lax.axis_size("col")
    gain = gain_row(level_row(level, table), ada)
    coarse_in = mm(tokens[...], win[...])
    coarse_in_out[...] = mm(own[...], win[...])
    cn = (rms_rows(coarse_in) * gain).astype(BF16)
    cn_ref[...] = (rms_rows(coarse_in) * gain)
    mine = cn_ref[pl.ds(pl.multiple_of(row * rows_each, rows_each), rows_each), :].astype(BF16)
    q, k, v = mm(mine, wqkv[0]), mm(cn, wqkv[1]), mm(cn, wqkv[2])
    low = low_lanes(q.shape)
    factor = jnp.where(low, scale[0], scale[1]) * (LOG2E / HEAD)
    q = q * lax.rsqrt(head_means(q) + EPS) * factor
    k = (k * lax.rsqrt(head_means(k) + EPS)).astype(BF16)
    wide = low_lanes(v.shape)
    v0 = jnp.where(wide, v, 1.0).astype(BF16)
    v1 = jnp.where(wide, 1.0, v).astype(BF16)
    q0 = jnp.where(low, q, 0.0).astype(BF16)
    q1 = jnp.where(low, 0.0, q).astype(BF16)
    a0 = mm(jnp.exp2(mm(q0, k, NT)).astype(BF16), v0)
    a1 = mm(jnp.exp2(mm(q1, k, NT)).astype(BF16), v1)
    sums = pltpu.roll(jnp.where(low, a1, a0), HEAD, 1)
    attended = (jnp.where(low, a0, a1) / sums).astype(BF16)
    part_out[...] = mm(attended, wout[...]).astype(BF16).reshape(part_out.shape)


def final_kernel(parts, coarse_in, post, out):
    branch = jnp.sum(parts[...].astype(F32), axis=0)
    out[...] = (coarse_in[...] + rms_rows(branch) * post[...]).astype(BF16)


def call(kernel, out_shape, args, smem=0, scratch=(), aliases=None, flops=0, name=None):
    vmem = pl.BlockSpec(memory_space=pltpu.VMEM)
    scalars = pl.BlockSpec(memory_space=pltpu.SMEM)
    moved = sum(a.size * a.dtype.itemsize for a in args)
    return pl.pallas_call(
        kernel,
        out_shape=out_shape,
        in_specs=[scalars] * smem + [vmem] * (len(args) - smem),
        out_specs=jax.tree.map(lambda _: vmem, out_shape),
        scratch_shapes=list(scratch),
        input_output_aliases=aliases or {},
        compiler_params=pltpu.CompilerParams(vmem_limit_bytes=VMEM_LIMIT),
        cost_estimate=pl.CostEstimate(flops=flops, bytes_accessed=moved, transcendentals=0),
        name=name,
    )(*args)


def body(
    image,
    noise_level,
    cond_table,
    ada_fine,
    fine_qkv,
    fine_scale,
    fine_out_w,
    fine_post,
    merge_w,
    coarse_in_w,
    ada_coarse,
    coarse_qkv,
    coarse_scale,
    coarse_out_w,
    coarse_post,
):
    shape = jax.ShapeDtypeStruct
    rows, cols, width = image.shape
    count = rows * cols
    n_row, n_col = lax.axis_size("row"), lax.axis_size("col")
    x = image.reshape(count, width)

    def swaps(n, odd):
        pairs = [(i, i + 1) for i in range(odd, n - 1, 2)]
        return pairs + [(j, i) for i, j in pairs]

    tile_flops = 4 * count * count * width * 4
    col_a = lax.ppermute(x, "col", swaps(n_col, 0))
    col_b = lax.ppermute(x, "col", swaps(n_col, 1))
    q0, q1, acc0, acc1, gain = call(
        own_kernel,
        (shape((count, width), BF16),) * 2 + (shape((count, width), F32),) * 2 + (shape((1, width), F32),),
        (noise_level, fine_scale, x, cond_table, ada_fine, fine_qkv),
        smem=2,
        flops=tile_flops,
        name="own_tile",
    )
    held, gain = lax.optimization_barrier((x, gain))
    three = jnp.stack([held, col_a, col_b])
    near = lax.ppermute(three, "row", swaps(n_row, 0))
    far = lax.ppermute(three, "row", swaps(n_row, 1))
    accs = (shape((count, width), F32),) * 2
    acc0, acc1 = call(
        col_kernel,
        accs,
        (col_a, col_b, gain, fine_qkv, q0, q1, acc0, acc1),
        flops=2 * tile_flops,
        name="col_tiles",
    )
    acc0, acc1 = call(
        near_kernel,
        accs,
        (near, gain, fine_qkv, q0, q1, acc0, acc1),
        flops=3 * tile_flops,
        name="near_row_tiles",
    )
    devices = n_row * n_col
    merge_width = merge_w.shape[1]
    fine_out, pooled = call(
        far_kernel,
        (shape((count, width), BF16), shape((devices, 4, merge_width), BF16)),
        (far, gain, fine_qkv, q0, q1, acc0, acc1, x, fine_out_w, fine_post[None], merge_w),
        scratch=[pltpu.VMEM((count, width), F32)] * 2,
        flops=3 * tile_flops,
        name="far_row_tiles",
    )
    tokens = lax.all_to_all(pooled, ("row", "col"), 0, 0, tiled=True)
    coarse_width = coarse_in_w.shape[1]
    own = 4
    parts, coarse_in = call(
        coarse_kernel,
        (shape((n_col, own, coarse_width), BF16), shape((own, coarse_width), F32)),
        (
            noise_level,
            coarse_scale,
            tokens.reshape(-1, merge_width),
            cond_table,
            ada_coarse,
            coarse_in_w,
            coarse_qkv,
            coarse_out_w,
            pooled[0],
        ),
        smem=2,
        scratch=[pltpu.VMEM((devices * own, coarse_width), F32)] * 2,
        name="coarse",
    )
    parts = lax.all_to_all(parts, "col", 0, 0, tiled=True)
    coarse_out = call(
        final_kernel,
        shape((own, coarse_width), BF16),
        (parts, coarse_in, coarse_post[None]),
        name="coarse_out",
    )
    pooled_rows, pooled_cols = rows // (2 * POOL), cols // (2 * POOL)
    return fine_out.reshape(rows, cols, width), coarse_out.reshape(pooled_rows, pooled_cols, coarse_width)


def solution(mesh):
    in_specs = (
        P(("noise", "row"), "col", None),
        P("noise"),
        P(),
        P(),
        P(),
        P(),
        P(),
        P(),
        P(),
        P(),
        P(),
        P(None, None, "col"),
        P("col"),
        P("col", None),
        P(),
    )
    out_specs = (P(("noise", "row"), "col", None), P(("noise", "row"), "col", None))
    return jax.shard_map(body, mesh=mesh, in_specs=in_specs, out_specs=out_specs, check_vma=False)
```

```python
import functools

import jax
import jax.numpy as jnp
from jax import lax
from jax.experimental import pallas as pl
from jax.experimental.pallas import tpu as pltpu
from jax.sharding import PartitionSpec as P

HEAD = 64
POOL = 8
EPS = 1e-06
LOG2E = 1.4426950408889634
QCHUNK = 256
VMEM_LIMIT = 40 * 1024 * 1024
NT = (((1,), (1,)), ((), ()))
NN = (((1,), (0,)), ((), ()))
F32 = jnp.float32
BF16 = jnp.bfloat16


def mm(a, b, dims=NN):
    return lax.dot_general(a, b, dims, preferred_element_type=F32)


def rms_rows(value):
    return value * lax.rsqrt(jnp.mean(value * value, axis=-1, keepdims=True) + EPS)


def head_means(value):
    width = value.shape[1]
    i = lax.broadcasted_iota(jnp.int32, (width, width), 0) // HEAD
    j = lax.broadcasted_iota(jnp.int32, (width, width), 1) // HEAD
    ones = jnp.where(i == j, 1.0 / HEAD, 0.0).astype(BF16)
    return mm((value * value).astype(BF16), ones)


def low_lanes(shape):
    return lax.broadcasted_iota(jnp.int32, shape, 1) < HEAD


def level_row(level_ref, table_ref):
    table = table_ref[...]
    ids = lax.broadcasted_iota(jnp.int32, table.shape, 0)
    return jnp.sum(jnp.where(ids == level_ref[0], table, 0.0), axis=0, keepdims=True)


def gain_row(cond, ada_ref):
    return 1.0 + lax.dot_general(
        cond, ada_ref[...], NN, precision=lax.Precision.HIGHEST, preferred_element_type=F32
    )


def tile_kv(x, gain, wkv, valid):
    width = x.shape[1]
    xn = (rms_rows(x.astype(F32)) * gain).astype(BF16)
    proj = mm(xn, wkv)
    k = proj[:, :width]
    k = (k * lax.rsqrt(head_means(k) + EPS)).astype(BF16)
    v = proj[:, width:]
    low = low_lanes(v.shape)
    v0 = jnp.where(low, v, valid).astype(BF16)
    v1 = jnp.where(low, valid, v).astype(BF16)
    return xn, k, v0, v1


def attend_tile(q_refs, k, vs, acc_refs, first):
    for start in range(0, q_refs[0].shape[0], QCHUNK):
        rows = pl.ds(start, QCHUNK)
        for q_ref, v, acc_ref in zip(q_refs, vs, acc_refs):
            p = jnp.exp2(mm(q_ref[rows, :], k, NT)).astype(BF16)
            part = mm(p, v)
            if first:
                acc_ref[rows, :] = part
            else:
                acc_ref[rows, :] += part


def fetch(pairs, sems):
    copies = [pltpu.make_async_copy(src, dst, sems.at[i]) for i, (src, dst) in enumerate(pairs)]
    for copy in copies:
        copy.start()
    return copies


def own_kernel(
    level,
    scale_hbm,
    x_hbm,
    table_hbm,
    ada_hbm,
    wqkv_hbm,
    q0,
    q1,
    acc0,
    acc1,
    gain_out,
    cond_out,
    wkv_out,
    scale,
    x,
    table,
    ada,
    wqkv,
    sems,
):
    copies = fetch(
        (
            (table_hbm, table),
            (ada_hbm, ada),
            (x_hbm, x),
            (wqkv_hbm, wqkv),
            (scale_hbm, scale),
        ),
        sems,
    )
    for copy in copies:
        copy.wait()
    width = x.shape[1]
    cond = level_row(level, table)
    gain = gain_row(cond, ada)
    cond_out[...] = cond
    gain_out[...] = gain
    wkv = wqkv[:, width:]
    wkv_out[...] = wkv
    xn, k, v0, v1 = tile_kv(x[...], gain, wkv, 1.0)
    q = mm(xn, wqkv[:, :width])
    low = low_lanes(q.shape)
    factor = jnp.where(low, scale[0], scale[1]) * (LOG2E / HEAD)
    q = q * lax.rsqrt(head_means(q) + EPS) * factor
    q0[...] = jnp.where(low, q, 0.0).astype(BF16)
    q1[...] = jnp.where(low, 0.0, q).astype(BF16)
    attend_tile((q0, q1), k, (v0, v1), (acc0, acc1), True)


def more_tiles(which, tiles, gain, wkv, q_refs, acc_refs):
    row, col = lax.axis_index("row"), lax.axis_index("col")
    row_ok = jnp.where((row > 0) & (row < lax.axis_size("row") - 1), 1.0, 0.0)
    col_ok = jnp.where((col > 0) & (col < lax.axis_size("col") - 1), 1.0, 0.0)
    flags = {
        "col": (1.0, col_ok),
        "near": (1.0, 1.0, col_ok),
        "far": (row_ok, row_ok, row_ok * col_ok),
    }
    for at, valid in enumerate(flags[which]):
        _, k, v0, v1 = tile_kv(tiles[at][...], gain[...], wkv[...], valid)
        attend_tile(q_refs, k, (v0, v1), acc_refs, at == 0)


def col_kernel(a, b, gain, wkv, q0, q1, acc0, acc1):
    more_tiles("col", (a, b), gain, wkv, (q0, q1), (acc0, acc1))


def near_kernel(tiles, gain, wkv, q0, q1, acc0, acc1):
    more_tiles("near", [tiles.at[i] for i in range(3)], gain, wkv, (q0, q1), (acc0, acc1))


def far_kernel(
    tiles,
    gain,
    wkv,
    q0,
    q1,
    own0,
    own1,
    col0,
    col1,
    near0,
    near1,
    x_hbm,
    wout_hbm,
    post_hbm,
    wmerge_hbm,
    out_hbm,
    pooled,
    pooled_all,
    acc0,
    acc1,
    x,
    wout,
    post,
    wmerge,
    out,
    sems,
):
    copies = fetch(
        ((x_hbm, x), (wout_hbm, wout), (post_hbm, post), (wmerge_hbm, wmerge)), sems
    )
    more_tiles("far", [tiles.at[i] for i in range(3)], gain, wkv, (q0, q1), (acc0, acc1))
    for copy in copies:
        copy.wait()
    tokens, width = x.shape
    low = low_lanes((tokens, width))
    a0 = (own0[...] + col0[...]) + (near0[...] + acc0[...])
    a1 = (own1[...] + col1[...]) + (near1[...] + acc1[...])
    sums = pltpu.roll(jnp.where(low, a1, a0), HEAD, 1)
    attended = (jnp.where(low, a0, a1) / sums).astype(BF16)
    branch = mm(attended, wout[...])
    result = (x[...].astype(F32) + rms_rows(branch) * post[...]).astype(BF16)
    out[...] = result
    store = pltpu.make_async_copy(out, out_hbm, sems.at[4])
    store.start()
    side = 32
    group = lax.broadcasted_iota(jnp.int32, (16, tokens), 0)
    token = lax.broadcasted_iota(jnp.int32, (16, tokens), 1)
    i, j = token // side, token % side
    place = ((i % 2) * 2 + j % 2) * 4 + (i // (2 * POOL)) * 2 + j // (2 * POOL)
    pick = jnp.where(group == place, 1.0 / (POOL * POOL), 0.0).astype(BF16)
    means = mm(pick, result)
    high = means.astype(BF16)
    rest = (means - high.astype(F32)).astype(BF16)
    total = jnp.zeros((4, wmerge.shape[1]), F32)
    for part in range(4):
        w = wmerge[pl.ds(part * width, width), :]
        at = slice(4 * part, 4 * part + 4)
        total += mm(high[at], w) + mm(rest[at], w)
    total = total.astype(BF16)
    pooled[...] = total
    pooled_all[...] = jnp.broadcast_to(total[None], pooled_all.shape)
    store.wait()


def prepare_kernel(pooled, cond, ada, win, gain, coarse_in):
    gain[...] = gain_row(cond[...], ada)
    coarse_in[...] = mm(pooled[...], win[...])


def coarse_kernel(scale_hbm, tokens, gain, win, wqkv, wout, part_out, q_ref, scale, sems):
    (copy,) = fetch(((scale_hbm, scale),), sems)
    row = lax.axis_index("row")
    count = tokens.shape[0]
    rows_each = count // lax.axis_size("row")
    coarse_in = mm(tokens[...], win[...])
    cn = (rms_rows(coarse_in) * gain[...]).astype(BF16)
    qk = mm(cn, jnp.concatenate([wqkv[0], wqkv[1]], axis=1))
    width = wqkv.shape[2]
    k = qk[:, width:]
    v = mm(cn, wqkv[2])
    q_ref[...] = qk[:, :width]
    q = q_ref[pl.ds(pl.multiple_of(row * rows_each, rows_each), rows_each), :]
    copy.wait()
    low = low_lanes(q.shape)
    factor = jnp.where(low, scale[0], scale[1]) * (LOG2E / HEAD)
    q = q * lax.rsqrt(head_means(q) + EPS) * factor
    k = (k * lax.rsqrt(head_means(k) + EPS)).astype(BF16)
    wide = low_lanes(v.shape)
    v0 = jnp.where(wide, v, 1.0).astype(BF16)
    v1 = jnp.where(wide, 1.0, v).astype(BF16)
    q0 = jnp.where(low, q, 0.0).astype(BF16)
    q1 = jnp.where(low, 0.0, q).astype(BF16)
    a0 = mm(jnp.exp2(mm(q0, k, NT)).astype(BF16), v0)
    a1 = mm(jnp.exp2(mm(q1, k, NT)).astype(BF16), v1)
    sums = pltpu.roll(jnp.where(low, a1, a0), HEAD, 1)
    attended = (jnp.where(low, a0, a1) / sums).astype(BF16)
    part_out[...] = mm(attended, wout[...]).astype(BF16).reshape(part_out.shape)


def final_kernel(parts, coarse_in, post, out):
    branch = jnp.sum(parts[...].astype(F32), axis=0)
    result = (coarse_in[...] + rms_rows(branch) * post[...]).astype(BF16)
    each = out.shape[1]
    for at in range(out.shape[0]):
        out[at] = result[at * each : (at + 1) * each]


def call(kernel, out_shape, args, spaces, outs=None, scratch=(), flops=0, name=None):
    specs = {
        "s": pl.BlockSpec(memory_space=pltpu.SMEM),
        "v": pl.BlockSpec(memory_space=pltpu.VMEM),
        "h": pl.BlockSpec(memory_space=pltpu.HBM),
    }
    moved = sum(a.size * a.dtype.itemsize for a in args)
    args = [
        pltpu.with_memory_space_constraint(a, pltpu.HBM) if space == "h" else a
        for a, space in zip(args, spaces)
    ]
    return pl.pallas_call(
        kernel,
        out_shape=out_shape,
        in_specs=[specs[space] for space in spaces],
        out_specs=tuple(specs[space] for space in (outs or "v" * len(out_shape))),
        scratch_shapes=list(scratch),
        compiler_params=pltpu.CompilerParams(vmem_limit_bytes=VMEM_LIMIT),
        cost_estimate=pl.CostEstimate(flops=flops, bytes_accessed=moved, transcendentals=0),
        name=name,
    )(*args)


def body(
    image,
    noise_level,
    cond_table,
    ada_fine,
    fine_qkv,
    fine_scale,
    fine_out_w,
    fine_post,
    merge_w,
    coarse_in_w,
    ada_coarse,
    coarse_qkv,
    coarse_scale,
    coarse_out_w,
    coarse_post,
):
    shape = jax.ShapeDtypeStruct
    rows, cols, width = image.shape
    count = rows * cols
    n_row, n_col = lax.axis_size("row"), lax.axis_size("col")
    x = image.reshape(count, width)

    def swaps(n, odd):
        pairs = [(i, i + 1) for i in range(odd, n - 1, 2)]
        return pairs + [(j, i) for i, j in pairs]

    tile_flops = 4 * count * count * width * 4
    col_a = lax.ppermute(x, "col", swaps(n_col, 0))
    col_b = lax.ppermute(x, "col", swaps(n_col, 1))
    vmem, dma = pltpu.VMEM, pltpu.SemaphoreType.DMA
    accs = (shape((count, width), F32),) * 2
    q0, q1, own0, own1, gain, cond, wkv = call(
        own_kernel,
        (shape((count, width), BF16),) * 2
        + accs
        + (
            shape((1, width), F32),
            shape((1, cond_table.shape[1]), F32),
            shape((width, 2 * width), BF16),
        ),
        (noise_level, fine_scale, x, cond_table, ada_fine, fine_qkv),
        "shhhhh",
        scratch=[
            pltpu.SMEM(fine_scale.shape, F32),
            vmem(x.shape, BF16),
            vmem(cond_table.shape, F32),
            vmem(ada_fine.shape, F32),
            vmem(fine_qkv.shape, BF16),
            dma((5,)),
        ],
        flops=tile_flops,
        name="own_tile",
    )
    held, gain = lax.optimization_barrier((x, gain))
    three = jnp.stack([held, col_a, col_b])
    near = lax.ppermute(three, "row", swaps(n_row, 0))
    far = lax.ppermute(three, "row", swaps(n_row, 1))
    col0, col1 = call(
        col_kernel,
        accs,
        (col_a, col_b, gain, wkv, q0, q1),
        "vvvvvv",
        flops=2 * tile_flops,
        name="col_tiles",
    )
    near0, near1 = call(
        near_kernel,
        accs,
        (near, gain, wkv, q0, q1),
        "vvvvv",
        flops=3 * tile_flops,
        name="near_row_tiles",
    )
    devices = n_row * n_col
    merge_width = merge_w.shape[1]
    own = 4
    post = fine_post[None]
    fine_out, pooled, pooled_all = call(
        far_kernel,
        (
            shape((count, width), BF16),
            shape((own, merge_width), BF16),
            shape((devices, own, merge_width), BF16),
        ),
        (far, gain, wkv, q0, q1, own0, own1, col0, col1, near0, near1)
        + (x, fine_out_w, post, merge_w),
        "v" * 11 + "hhhh",
        outs="hvv",
        scratch=[vmem((count, width), F32)] * 2
        + [
            vmem(x.shape, BF16),
            vmem(fine_out_w.shape, BF16),
            vmem(post.shape, F32),
            vmem(merge_w.shape, BF16),
            vmem(x.shape, BF16),
            dma((5,)),
        ],
        flops=3 * tile_flops,
        name="far_row_tiles",
    )
    tokens = lax.all_to_all(pooled_all, ("row", "col"), 0, 0, tiled=True)
    coarse_width = coarse_in_w.shape[1]
    coarse_gain, coarse_in = call(
        prepare_kernel,
        (shape((1, coarse_width), F32), shape((own, coarse_width), F32)),
        (pooled, cond, ada_coarse, coarse_in_w),
        "vvvv",
        name="coarse_prepare",
    )
    (parts,) = call(
        coarse_kernel,
        (shape((n_col, own, coarse_width), BF16),),
        (
            coarse_scale,
            tokens.reshape(-1, merge_width),
            coarse_gain,
            coarse_in_w,
            coarse_qkv,
            coarse_out_w,
        ),
        "hvvvvv",
        scratch=[
            vmem((devices * own, coarse_qkv.shape[2]), F32),
            pltpu.SMEM(coarse_scale.shape, F32),
            dma((1,)),
        ],
        name="coarse",
    )
    parts = lax.all_to_all(parts, "col", 0, 0, tiled=True)
    pooled_rows, pooled_cols = rows // (2 * POOL), cols // (2 * POOL)
    (coarse_out,) = call(
        final_kernel,
        (shape((pooled_rows, pooled_cols, coarse_width), BF16),),
        (parts, coarse_in, coarse_post[None]),
        "vvv",
        name="coarse_out",
    )
    return fine_out.reshape(rows, cols, width), coarse_out


def solution(mesh):
    in_specs = (
        P(("noise", "row"), "col", None),
        P("noise"),
        P(),
        P(),
        P(),
        P(),
        P(),
        P(),
        P(),
        P(),
        P(),
        P(None, None, "col"),
        P("col"),
        P("col", None),
        P(),
    )
    out_specs = (P(("noise", "row"), "col", None), P(("noise", "row"), "col", None))
    return jax.shard_map(body, mesh=mesh, in_specs=in_specs, out_specs=out_specs, check_vma=False)
```

```python
import functools

import jax
import jax.numpy as jnp
from jax import lax
from jax.experimental import pallas as pl
from jax.experimental.pallas import tpu as pltpu
from jax.sharding import PartitionSpec as P

HEAD = 64
POOL = 8
EPS = 1e-06
LOG2E = 1.4426950408889634
QCHUNK = 256
VMEM_LIMIT = 40 * 1024 * 1024
NT = (((1,), (1,)), ((), ()))
NN = (((1,), (0,)), ((), ()))
F32 = jnp.float32
BF16 = jnp.bfloat16


def mm(a, b, dims=NN):
    return lax.dot_general(a, b, dims, preferred_element_type=F32)


def rms_rows(value):
    return value * lax.rsqrt(jnp.mean(value * value, axis=-1, keepdims=True) + EPS)


def head_means(value):
    width = value.shape[1]
    i = lax.broadcasted_iota(jnp.int32, (width, width), 0) // HEAD
    j = lax.broadcasted_iota(jnp.int32, (width, width), 1) // HEAD
    ones = jnp.where(i == j, 1.0 / HEAD, 0.0).astype(BF16)
    return mm((value * value).astype(BF16), ones)


def low_lanes(shape):
    return lax.broadcasted_iota(jnp.int32, shape, 1) < HEAD


def level_row(level_ref, table_ref):
    table = table_ref[...]
    ids = lax.broadcasted_iota(jnp.int32, table.shape, 0)
    return jnp.sum(jnp.where(ids == level_ref[0], table, 0.0), axis=0, keepdims=True)


def gain_row(cond, ada_ref):
    return 1.0 + lax.dot_general(
        cond, ada_ref[...], NN, precision=lax.Precision.HIGHEST, preferred_element_type=F32
    )


def tile_kv(x, gain, wkv, valid):
    width = x.shape[1]
    xn = (rms_rows(x.astype(F32)) * (gain * valid)).astype(BF16)
    proj = mm(xn, wkv)
    k = proj[:, :width]
    k = (k * lax.rsqrt(head_means(k) + EPS)).astype(BF16)
    v = proj[:, width:]
    low = low_lanes(v.shape)
    v0 = jnp.where(low, v, valid).astype(BF16)
    v1 = jnp.where(low, valid, v).astype(BF16)
    return xn, k, v0, v1


def attend_tile(q_refs, k, vs, acc_refs, first):
    for start in range(0, q_refs[0].shape[0], QCHUNK):
        rows = pl.ds(start, QCHUNK)
        for q_ref, v, acc_ref in zip(q_refs, vs, acc_refs):
            p = jnp.exp2(mm(q_ref[rows, :], k, NT)).astype(BF16)
            part = mm(p, v)
            if first:
                acc_ref[rows, :] = part
            else:
                acc_ref[rows, :] += part


def fetch(pairs, sems):
    copies = [pltpu.make_async_copy(src, dst, sems.at[i]) for i, (src, dst) in enumerate(pairs)]
    for copy in copies:
        copy.start()
    return copies


def own_kernel(
    level,
    scale_hbm,
    x_hbm,
    table_hbm,
    ada_hbm,
    wqkv_hbm,
    post_hbm,
    near_tile,
    q0,
    q1,
    acc0,
    acc1,
    gain_out,
    cond_out,
    wkv_out,
    post_out,
    scale,
    x,
    table,
    ada,
    wqkv,
    sems,
):
    copies = fetch(
        (
            (table_hbm, table),
            (ada_hbm, ada),
            (x_hbm, x),
            (wqkv_hbm, wqkv),
            (scale_hbm, scale),
            (post_hbm, post_out),
        ),
        sems,
    )
    for copy in copies:
        copy.wait()
    width = x.shape[1]
    cond = level_row(level, table)
    gain = gain_row(cond, ada)
    cond_out[...] = cond
    gain_out[...] = gain
    wkv = wqkv[:, width:]
    wkv_out[...] = wkv
    xn, k, v0, v1 = tile_kv(x[...], gain, wkv, 1.0)
    q = mm(xn, wqkv[:, :width])
    low = low_lanes(q.shape)
    factor = jnp.where(low, scale[0], scale[1]) * (LOG2E / HEAD)
    q = q * lax.rsqrt(head_means(q) + EPS) * factor
    q0[...] = jnp.where(low, q, 0.0).astype(BF16)
    q1[...] = jnp.where(low, 0.0, q).astype(BF16)
    attend_tile((q0, q1), k, (v0, v1), (acc0, acc1), True)
    _, k, v0, v1 = tile_kv(near_tile[...], gain, wkv, 1.0)
    attend_tile((q0, q1), k, (v0, v1), (acc0, acc1), False)


def more_tiles(which, tiles, gain, wkv, q_refs, acc_refs):
    row, col = lax.axis_index("row"), lax.axis_index("col")
    row_ok = jnp.where((row > 0) & (row < lax.axis_size("row") - 1), 1.0, 0.0)
    col_ok = jnp.where((col > 0) & (col < lax.axis_size("col") - 1), 1.0, 0.0)
    flags = {
        "col": (1.0, col_ok),
        "near": (1.0, col_ok),
        "far": (row_ok, row_ok, row_ok * col_ok),
    }
    for at, valid in enumerate(flags[which]):
        _, k, v0, v1 = tile_kv(tiles[at][...], gain[...], wkv[...], valid)
        attend_tile(q_refs, k, (v0, v1), acc_refs, at == 0)


def col_kernel(a, b, gain, wkv, q0, q1, acc0, acc1):
    more_tiles("col", (a, b), gain, wkv, (q0, q1), (acc0, acc1))


def near_kernel(tiles, gain, wkv, q0, q1, acc0, acc1):
    more_tiles("near", [tiles.at[i] for i in range(2)], gain, wkv, (q0, q1), (acc0, acc1))


def far_kernel(
    tiles,
    gain,
    wkv,
    q0,
    q1,
    own0,
    own1,
    col0,
    col1,
    near0,
    near1,
    x,
    wout,
    post,
    wmerge,
    out,
    pooled,
    pooled_all,
    acc0,
    acc1,
):
    more_tiles("far", [tiles.at[i] for i in range(3)], gain, wkv, (q0, q1), (acc0, acc1))
    tokens, width = x.shape
    low = low_lanes((tokens, width))
    a0 = (own0[...] + col0[...]) + (near0[...] + acc0[...])
    a1 = (own1[...] + col1[...]) + (near1[...] + acc1[...])
    sums = pltpu.roll(jnp.where(low, a1, a0), HEAD, 1)
    attended = (jnp.where(low, a0, a1) / sums).astype(BF16)
    branch = mm(attended, wout[...])
    result = (x[...].astype(F32) + rms_rows(branch) * post[...]).astype(BF16)
    out[...] = result
    side = 32
    group = lax.broadcasted_iota(jnp.int32, (16, tokens), 0)
    token = lax.broadcasted_iota(jnp.int32, (16, tokens), 1)
    i, j = token // side, token % side
    place = ((i % 2) * 2 + j % 2) * 4 + (i // (2 * POOL)) * 2 + j // (2 * POOL)
    pick = jnp.where(group == place, 1.0 / (POOL * POOL), 0.0).astype(BF16)
    means = mm(pick, result)
    high = means.astype(BF16)
    rest = (means - high.astype(F32)).astype(BF16)
    total = jnp.zeros((4, wmerge.shape[1]), F32)
    for part in range(4):
        w = wmerge[pl.ds(part * width, width), :]
        at = slice(4 * part, 4 * part + 4)
        total += mm(high[at], w) + mm(rest[at], w)
    total = total.astype(BF16)
    pooled[...] = total
    pooled_all[...] = jnp.broadcast_to(total[None], pooled_all.shape)


def prepare_kernel(pooled, cond, ada, win, scale, gain, coarse_in, factor):
    low = low_lanes(factor.shape)
    factor[...] = jnp.where(low, scale[0:1, 0:1], scale[0:1, 1:2]) * (LOG2E / HEAD)
    gain[...] = gain_row(cond[...], ada)
    coarse_in[...] = mm(pooled[...], win[...])


def coarse_kernel(factor, tokens, gain, win, wqkv, wout, part_out, q_ref):
    row = lax.axis_index("row")
    count = tokens.shape[0]
    rows_each = count // lax.axis_size("row")
    coarse_in = mm(tokens[...], win[...])
    cn = (rms_rows(coarse_in) * gain[...]).astype(BF16)
    qk = mm(cn, jnp.concatenate([wqkv[0], wqkv[1]], axis=1))
    width = wqkv.shape[2]
    k = qk[:, width:]
    v = mm(cn, wqkv[2])
    q_ref[...] = qk[:, :width]
    q = q_ref[pl.ds(pl.multiple_of(row * rows_each, rows_each), rows_each), :]
    low = low_lanes(q.shape)
    q = q * lax.rsqrt(head_means(q) + EPS) * factor[...]
    k = (k * lax.rsqrt(head_means(k) + EPS)).astype(BF16)
    wide = low_lanes(v.shape)
    v0 = jnp.where(wide, v, 1.0).astype(BF16)
    v1 = jnp.where(wide, 1.0, v).astype(BF16)
    q0 = jnp.where(low, q, 0.0).astype(BF16)
    q1 = jnp.where(low, 0.0, q).astype(BF16)
    a0 = mm(jnp.exp2(mm(q0, k, NT)).astype(BF16), v0)
    a1 = mm(jnp.exp2(mm(q1, k, NT)).astype(BF16), v1)
    sums = pltpu.roll(jnp.where(low, a1, a0), HEAD, 1)
    attended = (jnp.where(low, a0, a1) / sums).astype(BF16)
    part_out[...] = mm(attended, wout[...]).astype(BF16).reshape(part_out.shape)


def final_kernel(parts, coarse_in, post, out):
    branch = jnp.sum(parts[...].astype(F32), axis=0)
    result = (coarse_in[...] + rms_rows(branch) * post[...]).astype(BF16)
    each = out.shape[1]
    for at in range(out.shape[0]):
        out[at] = result[at * each : (at + 1) * each]


def call(kernel, out_shape, args, spaces, scratch=(), flops=0, name=None):
    specs = {
        "s": pl.BlockSpec(memory_space=pltpu.SMEM),
        "v": pl.BlockSpec(memory_space=pltpu.VMEM),
        "h": pl.BlockSpec(memory_space=pltpu.HBM),
    }
    moved = sum(a.size * a.dtype.itemsize for a in args)
    args = [
        pltpu.with_memory_space_constraint(a, pltpu.HBM) if space == "h" else a
        for a, space in zip(args, spaces)
    ]
    return pl.pallas_call(
        kernel,
        out_shape=out_shape,
        in_specs=[specs[space] for space in spaces],
        out_specs=(specs["v"],) * len(out_shape),
        scratch_shapes=list(scratch),
        compiler_params=pltpu.CompilerParams(vmem_limit_bytes=VMEM_LIMIT),
        cost_estimate=pl.CostEstimate(flops=flops, bytes_accessed=moved, transcendentals=0),
        name=name,
    )(*args)


def body(
    image,
    noise_level,
    cond_table,
    ada_fine,
    fine_qkv,
    fine_scale,
    fine_out_w,
    fine_post,
    merge_w,
    coarse_in_w,
    ada_coarse,
    coarse_qkv,
    coarse_scale,
    coarse_out_w,
    coarse_post,
):
    shape = jax.ShapeDtypeStruct
    rows, cols, width = image.shape
    count = rows * cols
    n_row, n_col = lax.axis_size("row"), lax.axis_size("col")
    x = image.reshape(count, width)

    def swaps(n, odd):
        pairs = [(i, (i + 1) % n) for i in range(odd, n, 2)]
        return pairs + [(j, i) for i, j in pairs]

    ring = 2 * n_row if lax.axis_size("noise") % 2 == 0 else n_row
    far_pairs = [
        (start + i, start + j)
        for start in range(0, lax.axis_size("noise") * n_row, ring)
        for i, j in swaps(ring, 1)
    ]
    tile_flops = 4 * count * count * width * 4
    near_tile = lax.ppermute(x, "row", swaps(n_row, 0))
    col_a = lax.ppermute(x, "col", swaps(n_col, 0))
    col_b = lax.ppermute(x, "col", swaps(n_col, 1))
    vmem, dma = pltpu.VMEM, pltpu.SemaphoreType.DMA
    accs = (shape((count, width), F32),) * 2
    q0, q1, own0, own1, gain, cond, wkv, post = call(
        own_kernel,
        (shape((count, width), BF16),) * 2
        + accs
        + (
            shape((1, width), F32),
            shape((1, cond_table.shape[1]), F32),
            shape((width, 2 * width), BF16),
            shape((1, width), F32),
        ),
        (noise_level, fine_scale, x, cond_table, ada_fine, fine_qkv, fine_post[None], near_tile),
        "shhhhhhv",
        scratch=[
            pltpu.SMEM(fine_scale.shape, F32),
            vmem(x.shape, BF16),
            vmem(cond_table.shape, F32),
            vmem(ada_fine.shape, F32),
            vmem(fine_qkv.shape, BF16),
            dma((6,)),
        ],
        flops=2 * tile_flops,
        name="own_tile",
    )
    held, col_a, col_b, gain = lax.optimization_barrier((x, col_a, col_b, gain))
    three = jnp.stack([held, col_a, col_b])
    near = lax.ppermute(jnp.stack([col_a, col_b]), "row", swaps(n_row, 0))
    far = lax.ppermute(three, ("noise", "row"), far_pairs)
    col0, col1 = call(
        col_kernel,
        accs,
        (col_a, col_b, gain, wkv, q0, q1),
        "vvvvvv",
        flops=2 * tile_flops,
        name="col_tiles",
    )
    near0, near1 = call(
        near_kernel,
        accs,
        (near, gain, wkv, q0, q1),
        "vvvvv",
        flops=2 * tile_flops,
        name="near_row_tiles",
    )
    devices = n_row * n_col
    merge_width = merge_w.shape[1]
    own = 4
    fine_out, pooled, pooled_all = call(
        far_kernel,
        (
            shape((count, width), BF16),
            shape((own, merge_width), BF16),
            shape((devices, own, merge_width), BF16),
        ),
        (far, gain, wkv, q0, q1, own0, own1, col0, col1, near0, near1)
        + (x, fine_out_w, post, merge_w),
        "v" * 15,
        scratch=[vmem((count, width), F32)] * 2,
        flops=3 * tile_flops,
        name="far_row_tiles",
    )
    tokens = lax.all_to_all(pooled_all, ("row", "col"), 0, 0, tiled=True)
    coarse_width = coarse_in_w.shape[1]
    local_width = coarse_qkv.shape[2]
    coarse_gain, coarse_in, factor = call(
        prepare_kernel,
        (
            shape((1, coarse_width), F32),
            shape((own, coarse_width), F32),
            shape((1, local_width), F32),
        ),
        (pooled, cond, ada_coarse, coarse_in_w, coarse_scale[None]),
        "vvvvv",
        name="coarse_prepare",
    )
    (parts,) = call(
        coarse_kernel,
        (shape((n_col, own, coarse_width), BF16),),
        (
            factor,
            tokens.reshape(-1, merge_width),
            coarse_gain,
            coarse_in_w,
            coarse_qkv,
            coarse_out_w,
        ),
        "vvvvvv",
        scratch=[vmem((devices * own, local_width), F32)],
        name="coarse",
    )
    parts = lax.all_to_all(parts, "col", 0, 0, tiled=True)
    pooled_rows, pooled_cols = rows // (2 * POOL), cols // (2 * POOL)
    (coarse_out,) = call(
        final_kernel,
        (shape((pooled_rows, pooled_cols, coarse_width), BF16),),
        (parts, coarse_in, coarse_post[None]),
        "vvv",
        name="coarse_out",
    )
    return fine_out.reshape(rows, cols, width), coarse_out


def solution(mesh):
    in_specs = (
        P(("noise", "row"), "col", None),
        P("noise"),
        P(),
        P(),
        P(),
        P(),
        P(),
        P(),
        P(),
        P(),
        P(),
        P(None, None, "col"),
        P("col"),
        P("col", None),
        P(),
    )
    out_specs = (P(("noise", "row"), "col", None), P(("noise", "row"), "col", None))
    return jax.shard_map(body, mesh=mesh, in_specs=in_specs, out_specs=out_specs, check_vma=False)
```

```python
import functools

import jax
import jax.numpy as jnp
from jax import lax
from jax.experimental import pallas as pl
from jax.experimental.pallas import tpu as pltpu
from jax.sharding import PartitionSpec as P

HEAD = 64
POOL = 8
EPS = 1e-06
LOG2E = 1.4426950408889634
QCHUNK = 256
VMEM_LIMIT = 40 * 1024 * 1024
NT = (((1,), (1,)), ((), ()))
NN = (((1,), (0,)), ((), ()))
F32 = jnp.float32
BF16 = jnp.bfloat16


def mm(a, b, dims=NN):
    return lax.dot_general(a, b, dims, preferred_element_type=F32)


def rms_rows(value):
    return value * lax.rsqrt(jnp.mean(value * value, axis=-1, keepdims=True) + EPS)


def head_rms(value):
    low = low_lanes(value.shape)
    square = value * value
    first = jnp.sum(jnp.where(low, square, 0.0), axis=-1, keepdims=True)
    second = jnp.sum(jnp.where(low, 0.0, square), axis=-1, keepdims=True)
    first = lax.rsqrt(first * (1.0 / HEAD) + EPS)
    second = lax.rsqrt(second * (1.0 / HEAD) + EPS)
    return value * jnp.where(low, first, second)


def low_lanes(shape):
    return lax.broadcasted_iota(jnp.int32, shape, 1) < HEAD


def level_row(level_ref, table_ref):
    table = table_ref[...]
    ids = lax.broadcasted_iota(jnp.int32, table.shape, 0)
    return jnp.sum(jnp.where(ids == level_ref[0], table, 0.0), axis=0, keepdims=True)


def gain_row(cond, ada_ref):
    return 1.0 + lax.dot_general(
        cond, ada_ref[...], NN, precision=lax.Precision.HIGHEST, preferred_element_type=F32
    )


def tile_kv(x, gain, wkv, valid):
    width = x.shape[1]
    xn = (rms_rows(x.astype(F32)) * (gain * valid)).astype(BF16)
    proj = mm(xn, wkv)
    k = head_rms(proj[:, :width]).astype(BF16)
    v = proj[:, width:]
    low = low_lanes(v.shape)
    v0 = jnp.where(low, v, valid).astype(BF16)
    v1 = jnp.where(low, valid, v).astype(BF16)
    return xn, k, v0, v1


def attend_tile(q_refs, k, vs, acc_refs, first):
    for start in range(0, q_refs[0].shape[0], QCHUNK):
        rows = pl.ds(start, QCHUNK)
        for q_ref, v, acc_ref in zip(q_refs, vs, acc_refs):
            p = jnp.exp2(mm(q_ref[rows, :], k, NT)).astype(BF16)
            part = mm(p, v)
            if first:
                acc_ref[rows, :] = part
            else:
                acc_ref[rows, :] += part


def fetch(pairs, sems):
    copies = [pltpu.make_async_copy(src, dst, sems.at[i]) for i, (src, dst) in enumerate(pairs)]
    for copy in copies:
        copy.start()
    return copies


def own_kernel(
    level,
    scale_hbm,
    x_hbm,
    table_hbm,
    ada_hbm,
    wqkv_hbm,
    post_hbm,
    near_tile,
    q0,
    q1,
    acc0,
    acc1,
    gain_out,
    cond_out,
    wkv_out,
    post_out,
    scale,
    x,
    table,
    ada,
    wqkv,
    sems,
):
    copies = fetch(
        (
            (table_hbm, table),
            (ada_hbm, ada),
            (x_hbm, x),
            (wqkv_hbm, wqkv),
            (scale_hbm, scale),
            (post_hbm, post_out),
        ),
        sems,
    )
    for copy in copies:
        copy.wait()
    width = x.shape[1]
    cond = level_row(level, table)
    turned = table[...].T
    ids = lax.broadcasted_iota(jnp.int32, turned.shape, 1)
    column = jnp.sum(jnp.where(ids == level[0], turned, 0.0), axis=1, keepdims=True)
    gain = 1.0 + jnp.sum(column * ada[...], axis=0, keepdims=True)
    cond_out[...] = cond
    gain_out[...] = gain
    wkv = wqkv[:, width:]
    wkv_out[...] = wkv
    xn, k, v0, v1 = tile_kv(x[...], gain, wkv, 1.0)
    q = mm(xn, wqkv[:, :width])
    low = low_lanes(q.shape)
    factor = jnp.where(low, scale[0], scale[1]) * (LOG2E / HEAD)
    q = head_rms(q) * factor
    q0[...] = jnp.where(low, q, 0.0).astype(BF16)
    q1[...] = jnp.where(low, 0.0, q).astype(BF16)
    _, near_k, near_v0, near_v1 = tile_kv(near_tile[...], gain, wkv, 1.0)
    attend_tile((q0, q1), k, (v0, v1), (acc0, acc1), True)
    attend_tile((q0, q1), near_k, (near_v0, near_v1), (acc0, acc1), False)


def more_tiles(which, tiles, gain, wkv, q_refs, acc_refs):
    row, col = lax.axis_index("row"), lax.axis_index("col")
    row_ok = jnp.where((row > 0) & (row < lax.axis_size("row") - 1), 1.0, 0.0)
    col_ok = jnp.where((col > 0) & (col < lax.axis_size("col") - 1), 1.0, 0.0)
    flags = {
        "col": (1.0, col_ok),
        "near": (1.0, col_ok),
        "far": (row_ok, row_ok, row_ok * col_ok),
    }
    held = [
        tile_kv(tile[...], gain[...], wkv[...], valid) for tile, valid in zip(tiles, flags[which])
    ]
    for at, (_, k, v0, v1) in enumerate(held):
        attend_tile(q_refs, k, (v0, v1), acc_refs, at == 0)


def col_kernel(a, b, gain, wkv, q0, q1, acc0, acc1):
    more_tiles("col", (a, b), gain, wkv, (q0, q1), (acc0, acc1))


def near_kernel(tiles, gain, wkv, q0, q1, acc0, acc1):
    more_tiles("near", [tiles.at[i] for i in range(2)], gain, wkv, (q0, q1), (acc0, acc1))


def far_kernel(
    tiles,
    gain,
    wkv,
    q0,
    q1,
    own0,
    own1,
    col0,
    col1,
    near0,
    near1,
    x,
    wout,
    post,
    wmerge,
    out,
    pooled,
    pooled_all,
    acc0,
    acc1,
):
    more_tiles("far", [tiles.at[i] for i in range(3)], gain, wkv, (q0, q1), (acc0, acc1))
    tokens, width = x.shape
    low = low_lanes((tokens, width))
    a0 = (own0[...] + col0[...]) + (near0[...] + acc0[...])
    a1 = (own1[...] + col1[...]) + (near1[...] + acc1[...])
    sums = pltpu.roll(jnp.where(low, a1, a0), HEAD, 1)
    attended = (jnp.where(low, a0, a1) / sums).astype(BF16)
    branch = mm(attended, wout[...])
    result = (x[...].astype(F32) + rms_rows(branch) * post[...]).astype(BF16)
    out[...] = result
    side = 32
    group = lax.broadcasted_iota(jnp.int32, (16, tokens), 0)
    token = lax.broadcasted_iota(jnp.int32, (16, tokens), 1)
    i, j = token // side, token % side
    place = ((i % 2) * 2 + j % 2) * 4 + (i // (2 * POOL)) * 2 + j // (2 * POOL)
    pick = jnp.where(group == place, 1.0 / (POOL * POOL), 0.0).astype(BF16)
    means = mm(pick, result)
    high = means.astype(BF16)
    rest = (means - high.astype(F32)).astype(BF16)
    total = jnp.zeros((4, wmerge.shape[1]), F32)
    for part in range(4):
        w = wmerge[pl.ds(part * width, width), :]
        at = slice(4 * part, 4 * part + 4)
        total += mm(high[at], w) + mm(rest[at], w)
    total = total.astype(BF16)
    pooled[...] = total
    pooled_all[...] = jnp.broadcast_to(total[None], pooled_all.shape)


def prepare_kernel(pooled, cond, ada, win, scale, gain, coarse_in, factor):
    low = low_lanes(factor.shape)
    factor[...] = jnp.where(low, scale[0:1, 0:1], scale[0:1, 1:2]) * (LOG2E / HEAD)
    gain[...] = gain_row(cond[...], ada)
    coarse_in[...] = mm(pooled[...], win[...])


def coarse_kernel(factor, tokens, gain, win, wqkv, wout, part_out, q_ref):
    row = lax.axis_index("row")
    count = tokens.shape[0]
    rows_each = count // lax.axis_size("row")
    coarse_in = mm(tokens[...], win[...])
    cn = (rms_rows(coarse_in) * gain[...]).astype(BF16)
    qk = mm(cn, jnp.concatenate([wqkv[0], wqkv[1]], axis=1))
    width = wqkv.shape[2]
    k = qk[:, width:]
    v = mm(cn, wqkv[2])
    q_ref[...] = qk[:, :width]
    q = q_ref[pl.ds(pl.multiple_of(row * rows_each, rows_each), rows_each), :]
    low = low_lanes(q.shape)
    q = head_rms(q) * factor[...]
    k = head_rms(k).astype(BF16)
    wide = low_lanes(v.shape)
    v0 = jnp.where(wide, v, 1.0).astype(BF16)
    v1 = jnp.where(wide, 1.0, v).astype(BF16)
    q0 = jnp.where(low, q, 0.0).astype(BF16)
    q1 = jnp.where(low, 0.0, q).astype(BF16)
    a0 = mm(jnp.exp2(mm(q0, k, NT)).astype(BF16), v0)
    a1 = mm(jnp.exp2(mm(q1, k, NT)).astype(BF16), v1)
    sums = pltpu.roll(jnp.where(low, a1, a0), HEAD, 1)
    attended = (jnp.where(low, a0, a1) / sums).astype(BF16)
    part_out[...] = mm(attended, wout[...]).astype(BF16).reshape(part_out.shape)


def final_kernel(parts, coarse_in, post, out):
    branch = jnp.sum(parts[...].astype(F32), axis=0)
    result = (coarse_in[...] + rms_rows(branch) * post[...]).astype(BF16)
    each = out.shape[1]
    for at in range(out.shape[0]):
        out[at] = result[at * each : (at + 1) * each]


def call(kernel, out_shape, args, spaces, scratch=(), flops=0, name=None):
    specs = {
        "s": pl.BlockSpec(memory_space=pltpu.SMEM),
        "v": pl.BlockSpec(memory_space=pltpu.VMEM),
        "h": pl.BlockSpec(memory_space=pltpu.HBM),
    }
    moved = sum(a.size * a.dtype.itemsize for a in args)
    args = [
        pltpu.with_memory_space_constraint(a, pltpu.HBM) if space == "h" else a
        for a, space in zip(args, spaces)
    ]
    return pl.pallas_call(
        kernel,
        out_shape=out_shape,
        in_specs=[specs[space] for space in spaces],
        out_specs=(specs["v"],) * len(out_shape),
        scratch_shapes=list(scratch),
        compiler_params=pltpu.CompilerParams(vmem_limit_bytes=VMEM_LIMIT),
        cost_estimate=pl.CostEstimate(flops=flops, bytes_accessed=moved, transcendentals=0),
        name=name,
    )(*args)


def body(
    image,
    noise_level,
    cond_table,
    ada_fine,
    fine_qkv,
    fine_scale,
    fine_out_w,
    fine_post,
    merge_w,
    coarse_in_w,
    ada_coarse,
    coarse_qkv,
    coarse_scale,
    coarse_out_w,
    coarse_post,
):
    shape = jax.ShapeDtypeStruct
    rows, cols, width = image.shape
    count = rows * cols
    n_row, n_col = lax.axis_size("row"), lax.axis_size("col")
    x = image.reshape(count, width)

    def swaps(n, odd):
        pairs = [(i, (i + 1) % n) for i in range(odd, n, 2)]
        return pairs + [(j, i) for i, j in pairs]

    ring = 2 * n_row if lax.axis_size("noise") % 2 == 0 else n_row
    far_pairs = [
        (start + i, start + j)
        for start in range(0, lax.axis_size("noise") * n_row, ring)
        for i, j in swaps(ring, 1)
    ]
    tile_flops = 4 * count * count * width * 4
    near_tile = lax.ppermute(x, "row", swaps(n_row, 0))
    col_a = lax.ppermute(x, "col", swaps(n_col, 0))
    col_b = lax.ppermute(x, "col", swaps(n_col, 1))
    vmem, dma = pltpu.VMEM, pltpu.SemaphoreType.DMA
    accs = (shape((count, width), F32),) * 2
    q0, q1, own0, own1, gain, cond, wkv, post = call(
        own_kernel,
        (shape((count, width), BF16),) * 2
        + accs
        + (
            shape((1, width), F32),
            shape((1, cond_table.shape[1]), F32),
            shape((width, 2 * width), BF16),
            shape((1, width), F32),
        ),
        (noise_level, fine_scale, x, cond_table, ada_fine, fine_qkv, fine_post[None], near_tile),
        "shhhhhhv",
        scratch=[
            pltpu.SMEM(fine_scale.shape, F32),
            vmem(x.shape, BF16),
            vmem(cond_table.shape, F32),
            vmem(ada_fine.shape, F32),
            vmem(fine_qkv.shape, BF16),
            dma((6,)),
        ],
        flops=2 * tile_flops,
        name="own_tile",
    )
    held, col_a, col_b, gain = lax.optimization_barrier((x, col_a, col_b, gain))
    three = jnp.stack([held, col_a, col_b])
    near = lax.ppermute(jnp.stack([col_a, col_b]), "row", swaps(n_row, 0))
    far = lax.ppermute(three, ("noise", "row"), far_pairs)
    col0, col1 = call(
        col_kernel,
        accs,
        (col_a, col_b, gain, wkv, q0, q1),
        "vvvvvv",
        flops=2 * tile_flops,
        name="col_tiles",
    )
    near0, near1 = call(
        near_kernel,
        accs,
        (near, gain, wkv, q0, q1),
        "vvvvv",
        flops=2 * tile_flops,
        name="near_row_tiles",
    )
    devices = n_row * n_col
    merge_width = merge_w.shape[1]
    own = 4
    fine_out, pooled, pooled_all = call(
        far_kernel,
        (
            shape((count, width), BF16),
            shape((own, merge_width), BF16),
            shape((devices, own, merge_width), BF16),
        ),
        (far, gain, wkv, q0, q1, own0, own1, col0, col1, near0, near1)
        + (x, fine_out_w, post, merge_w),
        "v" * 15,
        scratch=[vmem((count, width), F32)] * 2,
        flops=3 * tile_flops,
        name="far_row_tiles",
    )
    tokens = lax.all_to_all(pooled_all, ("row", "col"), 0, 0, tiled=True)
    coarse_width = coarse_in_w.shape[1]
    local_width = coarse_qkv.shape[2]
    coarse_gain, coarse_in, factor = call(
        prepare_kernel,
        (
            shape((1, coarse_width), F32),
            shape((own, coarse_width), F32),
            shape((1, local_width), F32),
        ),
        (pooled, cond, ada_coarse, coarse_in_w, coarse_scale[None]),
        "vvvvv",
        name="coarse_prepare",
    )
    (parts,) = call(
        coarse_kernel,
        (shape((n_col, own, coarse_width), BF16),),
        (
            factor,
            tokens.reshape(-1, merge_width),
            coarse_gain,
            coarse_in_w,
            coarse_qkv,
            coarse_out_w,
        ),
        "vvvvvv",
        scratch=[vmem((devices * own, local_width), F32)],
        name="coarse",
    )
    parts = lax.all_to_all(parts, "col", 0, 0, tiled=True)
    pooled_rows, pooled_cols = rows // (2 * POOL), cols // (2 * POOL)
    (coarse_out,) = call(
        final_kernel,
        (shape((pooled_rows, pooled_cols, coarse_width), BF16),),
        (parts, coarse_in, coarse_post[None]),
        "vvv",
        name="coarse_out",
    )
    return fine_out.reshape(rows, cols, width), coarse_out


def solution(mesh):
    in_specs = (
        P(("noise", "row"), "col", None),
        P("noise"),
        P(),
        P(),
        P(),
        P(),
        P(),
        P(),
        P(),
        P(),
        P(),
        P(None, None, "col"),
        P("col"),
        P("col", None),
        P(),
    )
    out_specs = (P(("noise", "row"), "col", None), P(("noise", "row"), "col", None))
    return jax.shard_map(body, mesh=mesh, in_specs=in_specs, out_specs=out_specs, check_vma=False)
```

```python
import functools

import jax
import jax.numpy as jnp
from jax import lax
from jax.experimental import pallas as pl
from jax.experimental.pallas import tpu as pltpu
from jax.sharding import PartitionSpec as P

HEAD = 64
POOL = 8
EPS = 1e-06
LOG2E = 1.4426950408889634
QCHUNK = 256
VMEM_LIMIT = 40 * 1024 * 1024
NT = (((1,), (1,)), ((), ()))
NN = (((1,), (0,)), ((), ()))
F32 = jnp.float32
BF16 = jnp.bfloat16


def mm(a, b, dims=NN):
    return lax.dot_general(a, b, dims, preferred_element_type=F32)


def rms_rows(value):
    return value * lax.rsqrt(jnp.mean(value * value, axis=-1, keepdims=True) + EPS)


def head_rms(value):
    low = low_lanes(value.shape)
    square = value * value
    first = jnp.sum(jnp.where(low, square, 0.0), axis=-1, keepdims=True)
    second = jnp.sum(jnp.where(low, 0.0, square), axis=-1, keepdims=True)
    first = lax.rsqrt(first * (1.0 / HEAD) + EPS)
    second = lax.rsqrt(second * (1.0 / HEAD) + EPS)
    return value * jnp.where(low, first, second)


def low_lanes(shape):
    return lax.broadcasted_iota(jnp.int32, shape, 1) < HEAD


def level_row(level_ref, table_ref):
    table = table_ref[...]
    ids = lax.broadcasted_iota(jnp.int32, table.shape, 0)
    return jnp.sum(jnp.where(ids == level_ref[0], table, 0.0), axis=0, keepdims=True)


def gain_row(cond, ada_ref):
    return 1.0 + lax.dot_general(
        cond, ada_ref[...], NN, precision=lax.Precision.HIGHEST, preferred_element_type=F32
    )


def tile_kv(x, gain, wkv, valid):
    width = x.shape[1]
    xn = (rms_rows(x.astype(F32)) * (gain * valid)).astype(BF16)
    proj = mm(xn, wkv)
    k = head_rms(proj[:, :width]).astype(BF16)
    v = proj[:, width:].astype(BF16)
    low = low_lanes(v.shape)
    flags = jnp.full(v.shape, valid, F32).astype(BF16)
    v0 = jnp.where(low, v, flags)
    v1 = jnp.where(low, flags, v)
    return xn, k, v0, v1


def attend_tile(q_refs, k, vs, acc_refs, first):
    for start in range(0, q_refs[0].shape[0], QCHUNK):
        rows = pl.ds(start, QCHUNK)
        for q_ref, v, acc_ref in zip(q_refs, vs, acc_refs):
            p = jnp.exp2(mm(q_ref[rows, :], k, NT)).astype(BF16)
            part = mm(p, v)
            if first:
                acc_ref[rows, :] = part
            else:
                acc_ref[rows, :] += part


def own_kernel(
    level,
    scale,
    x,
    table,
    ada,
    wqkv,
    post,
    near_tile,
    q0,
    q1,
    acc0,
    acc1,
    gain_out,
    cond_out,
    wkv_out,
    post_out,
):
    post_out[...] = post[...]
    width = x.shape[1]
    cond = level_row(level, table)
    turned = table[...].T
    ids = lax.broadcasted_iota(jnp.int32, turned.shape, 1)
    column = jnp.sum(jnp.where(ids == level[0], turned, 0.0), axis=1, keepdims=True)
    gain = 1.0 + jnp.sum(column * ada[...], axis=0, keepdims=True)
    cond_out[...] = cond
    gain_out[...] = gain
    wkv = wqkv[:, width:]
    wkv_out[...] = wkv
    xn, k, v0, v1 = tile_kv(x[...], gain, wkv, 1.0)
    q = mm(xn, wqkv[:, :width])
    low = low_lanes(q.shape)
    factor = jnp.where(low, scale[0], scale[1]) * (LOG2E / HEAD)
    q = head_rms(q) * factor
    q0[...] = jnp.where(low, q, 0.0).astype(BF16)
    q1[...] = jnp.where(low, 0.0, q).astype(BF16)
    _, near_k, near_v0, near_v1 = tile_kv(near_tile[...], gain, wkv, 1.0)
    attend_tile((q0, q1), k, (v0, v1), (acc0, acc1), True)
    attend_tile((q0, q1), near_k, (near_v0, near_v1), (acc0, acc1), False)


def more_tiles(which, tiles, gain, wkv, q_refs, acc_refs):
    row, col = lax.axis_index("row"), lax.axis_index("col")
    row_ok = jnp.where((row > 0) & (row < lax.axis_size("row") - 1), 1.0, 0.0)
    col_ok = jnp.where((col > 0) & (col < lax.axis_size("col") - 1), 1.0, 0.0)
    flags = {
        "col": (1.0, col_ok),
        "near": (1.0, col_ok),
        "far": (row_ok, row_ok, row_ok * col_ok),
    }
    held = [
        tile_kv(tile[...], gain[...], wkv[...], valid) for tile, valid in zip(tiles, flags[which])
    ]
    for at, (_, k, v0, v1) in enumerate(held):
        attend_tile(q_refs, k, (v0, v1), acc_refs, at == 0)


def col_kernel(a, b, gain, wkv, q0, q1, acc0, acc1):
    more_tiles("col", (a, b), gain, wkv, (q0, q1), (acc0, acc1))


def near_kernel(tiles, gain, wkv, q0, q1, acc0, acc1):
    more_tiles("near", [tiles.at[i] for i in range(2)], gain, wkv, (q0, q1), (acc0, acc1))


def far_kernel(
    tiles,
    gain,
    wkv,
    q0,
    q1,
    own0,
    own1,
    col0,
    col1,
    near0,
    near1,
    x,
    wout,
    post,
    wmerge,
    out,
    pooled,
    pooled_all,
    acc0,
    acc1,
):
    more_tiles("far", [tiles.at[i] for i in range(3)], gain, wkv, (q0, q1), (acc0, acc1))
    tokens, width = x.shape
    low = low_lanes((tokens, width))
    a0 = (own0[...] + col0[...]) + (near0[...] + acc0[...])
    a1 = (own1[...] + col1[...]) + (near1[...] + acc1[...])
    sums = pltpu.roll(jnp.where(low, a1, a0), HEAD, 1)
    attended = (jnp.where(low, a0, a1) / sums).astype(BF16)
    branch = mm(attended, wout[...])
    result = (x[...].astype(F32) + rms_rows(branch) * post[...]).astype(BF16)
    out[...] = result
    side = 32
    group = lax.broadcasted_iota(jnp.int32, (16, tokens), 0)
    token = lax.broadcasted_iota(jnp.int32, (16, tokens), 1)
    i, j = token // side, token % side
    place = ((i % 2) * 2 + j % 2) * 4 + (i // (2 * POOL)) * 2 + j // (2 * POOL)
    pick = jnp.where(group == place, 1.0 / (POOL * POOL), 0.0).astype(BF16)
    means = mm(pick, result)
    high = means.astype(BF16)
    rest = (means - high.astype(F32)).astype(BF16)
    total = jnp.zeros((4, wmerge.shape[1]), F32)
    for part in range(4):
        w = wmerge[pl.ds(part * width, width), :]
        at = slice(4 * part, 4 * part + 4)
        total += mm(high[at], w) + mm(rest[at], w)
    total = total.astype(BF16)
    pooled[...] = total
    pooled_all[...] = jnp.broadcast_to(total[None], pooled_all.shape)


def prepare_kernel(pooled, cond, ada, win, scale, gain, coarse_in, factor):
    low = low_lanes(factor.shape)
    factor[...] = jnp.where(low, scale[0:1, 0:1], scale[0:1, 1:2]) * (LOG2E / HEAD)
    gain[...] = gain_row(cond[...], ada)
    coarse_in[...] = mm(pooled[...], win[...])


def coarse_kernel(factor, tokens, gain, win, wqkv, wout, part_out, q_ref):
    row = lax.axis_index("row")
    count = tokens.shape[0]
    rows_each = count // lax.axis_size("row")
    coarse_in = mm(tokens[...], win[...])
    cn = (rms_rows(coarse_in) * gain[...]).astype(BF16)
    qk = mm(cn, jnp.concatenate([wqkv[0], wqkv[1]], axis=1))
    width = wqkv.shape[2]
    k = qk[:, width:]
    v = mm(cn, wqkv[2])
    q_ref[...] = qk[:, :width]
    q = q_ref[pl.ds(pl.multiple_of(row * rows_each, rows_each), rows_each), :]
    low = low_lanes(q.shape)
    q = head_rms(q) * factor[...]
    k = head_rms(k).astype(BF16)
    wide = low_lanes(v.shape)
    v0 = jnp.where(wide, v, 1.0).astype(BF16)
    v1 = jnp.where(wide, 1.0, v).astype(BF16)
    q0 = jnp.where(low, q, 0.0).astype(BF16)
    q1 = jnp.where(low, 0.0, q).astype(BF16)
    a0 = mm(jnp.exp2(mm(q0, k, NT)).astype(BF16), v0)
    a1 = mm(jnp.exp2(mm(q1, k, NT)).astype(BF16), v1)
    sums = pltpu.roll(jnp.where(low, a1, a0), HEAD, 1)
    attended = (jnp.where(low, a0, a1) / sums).astype(BF16)
    part_out[...] = mm(attended, wout[...]).astype(BF16).reshape(part_out.shape)


def final_kernel(parts, coarse_in, post, out):
    branch = jnp.sum(parts[...].astype(F32), axis=0)
    result = (coarse_in[...] + rms_rows(branch) * post[...]).astype(BF16)
    each = out.shape[1]
    for at in range(out.shape[0]):
        out[at] = result[at * each : (at + 1) * each]


def call(kernel, out_shape, args, spaces, scratch=(), flops=0, name=None):
    specs = {
        "s": pl.BlockSpec(memory_space=pltpu.SMEM),
        "v": pl.BlockSpec(memory_space=pltpu.VMEM),
        "h": pl.BlockSpec(memory_space=pltpu.VMEM),
        "t": pl.BlockSpec(memory_space=pltpu.SMEM),
    }
    moved = sum(a.size * a.dtype.itemsize for a in args)
    args = [
        pltpu.with_memory_space_constraint(a, pltpu.HBM) if space in "ht" else a
        for a, space in zip(args, spaces)
    ]
    return pl.pallas_call(
        kernel,
        out_shape=out_shape,
        in_specs=[specs[space] for space in spaces],
        out_specs=(specs["v"],) * len(out_shape),
        scratch_shapes=list(scratch),
        compiler_params=pltpu.CompilerParams(vmem_limit_bytes=VMEM_LIMIT),
        cost_estimate=pl.CostEstimate(flops=flops, bytes_accessed=moved, transcendentals=0),
        name=name,
    )(*args)


def body(
    image,
    noise_level,
    cond_table,
    ada_fine,
    fine_qkv,
    fine_scale,
    fine_out_w,
    fine_post,
    merge_w,
    coarse_in_w,
    ada_coarse,
    coarse_qkv,
    coarse_scale,
    coarse_out_w,
    coarse_post,
):
    shape = jax.ShapeDtypeStruct
    rows, cols, width = image.shape
    count = rows * cols
    n_row, n_col = lax.axis_size("row"), lax.axis_size("col")
    x = image.reshape(count, width)

    def swaps(n, odd):
        pairs = [(i, (i + 1) % n) for i in range(odd, n, 2)]
        return pairs + [(j, i) for i, j in pairs]

    ring = 2 * n_row if lax.axis_size("noise") % 2 == 0 else n_row
    far_pairs = [
        (start + i, start + j)
        for start in range(0, lax.axis_size("noise") * n_row, ring)
        for i, j in swaps(ring, 1)
    ]
    tile_flops = 4 * count * count * width * 4
    near_tile = lax.ppermute(x, "row", swaps(n_row, 0))
    col_a = lax.ppermute(x, "col", swaps(n_col, 0))
    col_b = lax.ppermute(x, "col", swaps(n_col, 1))
    vmem = pltpu.VMEM
    accs = (shape((count, width), F32),) * 2
    q0, q1, own0, own1, gain, cond, wkv, post = call(
        own_kernel,
        (shape((count, width), BF16),) * 2
        + accs
        + (
            shape((1, width), F32),
            shape((1, cond_table.shape[1]), F32),
            shape((width, 2 * width), BF16),
            shape((1, width), F32),
        ),
        (noise_level, fine_scale, x, cond_table, ada_fine, fine_qkv, fine_post[None], near_tile),
        "sthhhhhv",
        flops=2 * tile_flops,
        name="own_tile",
    )
    held, col_a, col_b, gain = lax.optimization_barrier((x, col_a, col_b, gain))
    three = jnp.stack([held, col_a, col_b])
    far = lax.ppermute(three, ("noise", "row"), far_pairs)
    near = lax.ppermute(jnp.stack([col_a, col_b]), "row", swaps(n_row, 0))
    col0, col1 = call(
        col_kernel,
        accs,
        (col_a, col_b, gain, wkv, q0, q1),
        "vvvvvv",
        flops=2 * tile_flops,
        name="col_tiles",
    )
    near0, near1 = call(
        near_kernel,
        accs,
        (near, gain, wkv, q0, q1),
        "vvvvv",
        flops=2 * tile_flops,
        name="near_row_tiles",
    )
    devices = n_row * n_col
    merge_width = merge_w.shape[1]
    own = 4
    fine_out, pooled, pooled_all = call(
        far_kernel,
        (
            shape((count, width), BF16),
            shape((own, merge_width), BF16),
            shape((devices, own, merge_width), BF16),
        ),
        (far, gain, wkv, q0, q1, own0, own1, col0, col1, near0, near1)
        + (x, fine_out_w, post, merge_w),
        "v" * 15,
        scratch=[vmem((count, width), F32)] * 2,
        flops=3 * tile_flops,
        name="far_row_tiles",
    )
    tokens = lax.all_to_all(pooled_all, ("row", "col"), 0, 0, tiled=True)
    coarse_width = coarse_in_w.shape[1]
    local_width = coarse_qkv.shape[2]
    coarse_gain, coarse_in, factor = call(
        prepare_kernel,
        (
            shape((1, coarse_width), F32),
            shape((own, coarse_width), F32),
            shape((1, local_width), F32),
        ),
        (pooled, cond, ada_coarse, coarse_in_w, coarse_scale[None]),
        "vvvvv",
        name="coarse_prepare",
    )
    (parts,) = call(
        coarse_kernel,
        (shape((n_col, own, coarse_width), BF16),),
        (
            factor,
            tokens.reshape(-1, merge_width),
            coarse_gain,
            coarse_in_w,
            coarse_qkv,
            coarse_out_w,
        ),
        "vvvvvv",
        scratch=[vmem((devices * own, local_width), F32)],
        name="coarse",
    )
    parts = lax.all_to_all(parts, "col", 0, 0, tiled=True)
    pooled_rows, pooled_cols = rows // (2 * POOL), cols // (2 * POOL)
    (coarse_out,) = call(
        final_kernel,
        (shape((pooled_rows, pooled_cols, coarse_width), BF16),),
        (parts, coarse_in, coarse_post[None]),
        "vvv",
        name="coarse_out",
    )
    return fine_out.reshape(rows, cols, width), coarse_out


def solution(mesh):
    in_specs = (
        P(("noise", "row"), "col", None),
        P("noise"),
        P(),
        P(),
        P(),
        P(),
        P(),
        P(),
        P(),
        P(),
        P(),
        P(None, None, "col"),
        P("col"),
        P("col", None),
        P(),
    )
    out_specs = (P(("noise", "row"), "col", None), P(("noise", "row"), "col", None))
    return jax.shard_map(body, mesh=mesh, in_specs=in_specs, out_specs=out_specs, check_vma=False)
```
